256 devices in a mesh: shots: 4 (over y), space: 64 (over z, x, core).
Axes of the slice: x: 4, y: 4, z: 8, core: 2. Of those that a mesh axis runs over, the one named last changes fastest.
Arguments:
- probes: bfloat16 [8, 64, 2, 1024, 8, 128], P('shots', None, None, 'space'), may hold values from -6 to 6
- sources: bfloat16 [8, 2, 1024, 8, 128], P('shots', None, 'space'), may hold values from -6 to 6
- sketch: bfloat16 [256, 64, 64], P('space'), may hold values from -6 to 6
- pairing: int32 [8], replicated, may hold values from 0 to 7, each once
Outputs:
- basis: bfloat16 [256, 64, 64], P('space', 'shots')
The draws below stay inside these ranges and needn't reach their ends.
Inputs may be any that keep to these rules, and one draw needn't show every extreme that they name: `pairing`: a permutation of the 8 shot groups.
All inputs are finite; a program needn't handle non-finite values.
Results may differ from the reference program's by a relative error of at most 0.013.
Values may be sent and summed in bfloat16 or wider, within the bound.
A program may use at most 64 MiB of HBM per device.

```python
import math
import jax
import jax.numpy as jnp
from jax import lax

R = 64
NT = 2
CY = 2
CZ = 32
GROUPS = 8
NXC = 256
NXF = 1024
FY = 8
FZ = 128


def block_levels(key, dims, shards, least, high):
    def one(axis_at, blocks):
        steps = jax.random.uniform(jax.random.fold_in(jax.random.fold_in(key, 6), axis_at), (blocks,), jnp.float32, least / len(shards), high / len(shards))
        return jnp.repeat(jnp.exp(steps), dims[axis_at] // blocks).reshape((-1,) + (1,) * (len(dims) - axis_at - 1))

    gain = one(*shards[0])
    for cut in shards[1:]:
        gain = gain * one(*cut)
    return gain


def gaussian(stream_key, dims, scale, reach, cuts=(), held_as=jnp.bfloat16):
    loudness = block_levels(stream_key, dims, cuts, -0.22, 0.18) if cuts else 1.0
    entries = jax.random.normal(stream_key, dims, jnp.float32) * scale * loudness
    return jnp.minimum(jnp.maximum(entries, -reach), reach).astype(held_as)


def setup_inputs(seed: int = 0) -> dict:
    key_of = jax.random.split(jax.random.key(seed), 5)
    return {
        "probes": gaussian(key_of[0], (GROUPS, R, NT, NXF, FY, FZ), 1.0, 6.0, ((0, 4), (3, 64))),
        "sources": gaussian(key_of[1], (GROUPS, NT, NXF, FY, FZ), 1.0, 6.0, ((0, 4), (2, 64))),
        "sketch": gaussian(key_of[2], (NXC, R, CY * CZ), 1.0, 6.0, ((0, 64),)),
        "pairing": jax.random.permutation(key_of[3], GROUPS).astype(jnp.int32),
    }


def spline_table(fine_count, coarse_count, fine_start, coarse_start):
    fine_pos = jnp.arange(fine_count, dtype=jnp.float32) + fine_start
    coarse_pos = jnp.arange(coarse_count, dtype=jnp.float32) + coarse_start
    distance = jnp.abs((fine_pos[:, None] + 0.5 - 4.0 * coarse_pos[None, :] - 2.0) / 4.0)
    inner_part = 2.0 / 3.0 - distance ** 2 + 0.5 * distance ** 3
    outer_part = jnp.maximum(2.0 - distance, 0.0) ** 3 / 6.0
    return jnp.where(distance < 1.0, inner_part, outer_part) / 4.0

def solve_coef(gram_mats, cross_mats):
    rank_size = gram_mats.shape[-1]
    trace_sum = jnp.trace(gram_mats, axis1=1, axis2=2)
    ridge_term = 0.01 * trace_sum / rank_size + 1e-06
    identity = jnp.eye(rank_size, dtype=jnp.float32)
    factor = jnp.linalg.cholesky(gram_mats + ridge_term[:, None, None] * identity)
    halfway = lax.linalg.triangular_solve(factor, cross_mats, left_side=True, lower=True)
    return lax.linalg.triangular_solve(factor, halfway, left_side=True, lower=True, transpose_a=True)

def merge_level(pieces, sketch, scaling):
    hi = lax.Precision.HIGHEST
    piece_wide = pieces.astype(jnp.float32)
    sketch_wide = sketch.astype(jnp.float32)
    gram_mats = jnp.einsum('pxay,pxby->pab', piece_wide, piece_wide, precision=hi)
    cross_mats = jnp.einsum('pxay,xby->pab', piece_wide, sketch_wide, precision=hi)
    coefficients = solve_coef(gram_mats, cross_mats).astype(jnp.bfloat16)
    term_sums = jnp.einsum('pxay,pab->pxby', piece_wide, coefficients.astype(jnp.float32), precision=hi)
    pair_count = pieces.shape[0] // 2
    term_sums = term_sums.reshape((pair_count, 2) + term_sums.shape[1:])
    return (scaling * (term_sums[:, 0] + term_sums[:, 1])).astype(jnp.bfloat16)

def reference(probes, sources, sketch, pairing):
    hi = lax.Precision.HIGHEST
    table_x = spline_table(NXF, NXC, 0, 0)
    table_y = spline_table(FY, CY, 0, 0)
    table_z = spline_table(FZ, CZ, 0, 0)

    def restrict_group(group_data):
        probe_wide = group_data[0].astype(jnp.float32)
        source_wide = group_data[1].astype(jnp.float32)
        images = jnp.einsum('atxyz,txyz->axyz', probe_wide, source_wide, precision=hi)
        images = jnp.einsum('axyz,zc->axyc', images, table_z, precision=hi)
        images = jnp.einsum('axyc,yd->axdc', images, table_y, precision=hi)
        images = jnp.einsum('axdc,xe->aedc', images, table_x, precision=hi)
        images = jnp.transpose(images, (1, 0, 2, 3)).reshape(NXC, R, CY * CZ)
        return images.astype(jnp.bfloat16)
    leaves = lax.map(restrict_group, (probes, sources))
    pieces = jnp.take(leaves, pairing, axis=0)
    scaling = math.sqrt(NXC * CY * CZ / R)
    while pieces.shape[0] > 1:
        pieces = merge_level(pieces, sketch, scaling)
    return pieces[0]
```

```python
import functools
import math

import jax
import jax.numpy as jnp
import numpy as np
from jax import lax
from jax.experimental import pallas as pl
from jax.experimental.pallas import tpu as pltpu
from jax.sharding import PartitionSpec as P

MESH = pl.DeviceIdType.MESH
F32 = jnp.float32
BF16 = jnp.bfloat16
HI = lax.Precision.HIGHEST
RANK = 64
LANES = 128


def spline_weight(distance):
    s = np.abs(distance / 4.0)
    inner = 2.0 / 3.0 - s**2 + 0.5 * s**3
    outer = np.maximum(2.0 - s, 0.0) ** 3 / 6.0
    return np.where(s < 1.0, inner, outer) / 4.0


def weight_tables(fine_x, fine_y, fine_z):
    coarse_x, coarse_y, coarse_z = fine_x // 4 + 4, fine_y // 4, fine_z // 4
    jx, jy, jz = np.arange(fine_x), np.arange(fine_y), np.arange(fine_z)
    ix, iy, iz = np.arange(coarse_x) - 2, np.arange(coarse_y), np.arange(coarse_z)
    wx = spline_weight(jx[None, :] + 0.5 - 4 * ix[:, None] - 2)
    wy = spline_weight(jy[None, :] + 0.5 - 4 * iy[:, None] - 2)
    wz = spline_weight(jz[:, None] + 0.5 - 4 * iz[None, :] - 2)
    wxy = np.einsum("ij,de->idje", wx, wy).reshape(coarse_x * coarse_y, fine_x * fine_y)
    wxy = np.concatenate([wxy, wxy], axis=1).astype(np.float32)
    high = wxy.astype(BF16)
    low = (wxy - high.astype(np.float32)).astype(BF16)
    side = 8
    block = np.zeros((side, fine_z, side, coarse_z), np.float32)
    for i in range(side):
        block[i, :, i, :] = wz
    block = block.reshape(side * fine_z, side * coarse_z).astype(BF16)
    return np.concatenate([high, low], axis=0), block


def restrict_kernel(p_ref, s_ref, wxy_ref, wz_ref, own_ref, up_ref, down_ref, t_ref):
    step = pl.program_id(1)
    chunk = p_ref.shape[1]
    src = s_ref[0].reshape(256, LANES)
    wxy = wxy_ref[...]
    for a in range(0, chunk, 2):
        left = p_ref[0, a].reshape(256, LANES) * src
        right = p_ref[0, a + 1].reshape(256, LANES) * src
        both = jnp.dot(wxy, jnp.concatenate([left, right], axis=1), preferred_element_type=F32)
        both = both[:16] + both[16:]
        row = pl.multiple_of((step * chunk + a) * 16, 32)
        t_ref[pl.ds(row, 16), :] = both[:, :LANES]
        t_ref[pl.ds(row + 16, 16), :] = both[:, LANES:]

    @pl.when(step == pl.num_programs(1) - 1)
    def _():
        wz = wz_ref[...]
        for half in range(2):
            parts = [t_ref[pl.ds(half * 8 + k, RANK, stride=16), :] for k in range(8)]
            x = jnp.concatenate([q.astype(BF16) for q in parts], axis=1)
            y = jnp.dot(x, wz, preferred_element_type=F32)
            if half == 0:
                down_ref[0] = y[:, :LANES].astype(BF16)
                own_ref[0, :, :LANES] = y[:, LANES:]
            else:
                own_ref[0, :, LANES:] = y[:, :LANES]
                up_ref[0] = y[:, LANES:].astype(BF16)


def nt(a, b, precision=None):
    return lax.dot_general(
        a, b, (((1,), (1,)), ((), ())), precision=precision, preferred_element_type=F32
    )


def exchange_kernel(
    shots, depth, owners,
    own_ref, up_ref, down_ref, sk_ref, pair_ref,
    all_ref, g_ref,
    halo, m_ref, rs, red, zb, fin,
    hs, hr, ys, yr, rss, rsr, zs, zr, gs, gr,
):
    me = lax.axis_index("shots")
    sp = lax.axis_index("space")
    count = depth * owners
    z = sp // owners
    o = lax.rem(sp, owners)
    right = lax.rem(sp + 1, count)
    left = lax.rem(sp + count - 1, count)
    group = shots * owners
    line = me * owners + o
    rows = 256 // owners

    barrier = pltpu.get_barrier_semaphore()
    for peer in (left, right):
        pl.semaphore_signal(barrier, inc=1, device_id=(me, peer), device_id_type=MESH)
    for d in range(1, depth):
        peer = lax.rem(z + d, depth) * owners + o
        pl.semaphore_signal(barrier, inc=1, device_id=(me, peer), device_id_type=MESH)
    for d in range(1, group):
        peer = lax.rem(line + d, group)
        pl.semaphore_signal(
            barrier,
            inc=1,
            device_id=(peer // owners, z * owners + lax.rem(peer, owners)),
            device_id_type=MESH,
        )
    pl.semaphore_wait(barrier, 2 + depth - 1 + group - 1)

    def send(src, dst, ssem, rsem, target):
        copy = pltpu.make_async_remote_copy(
            src_ref=src, dst_ref=dst, send_sem=ssem, recv_sem=rsem,
            device_id=target, device_id_type=MESH,
        )
        copy.start()
        return copy

    copies = [
        send(up_ref, halo.at[0], hs.at[0], hr.at[0], (me, right)),
        send(down_ref, halo.at[1], hs.at[1], hr.at[1], (me, left)),
    ]
    for c in copies:
        c.wait()
    below = jnp.where(sp > 0, halo[0].astype(F32), 0.0)
    above = jnp.where(sp < count - 1, halo[1].astype(F32), 0.0)
    lead = (own_ref[:, :, :LANES] + below).astype(BF16)
    tail = (own_ref[:, :, LANES:] + above).astype(BF16)
    all_ref[pl.ds(2 * me, 2), :, :LANES] = lead
    all_ref[pl.ds(2 * me, 2), :, LANES:] = tail

    copies = []
    for d in range(1, shots):
        peer = lax.rem(me + d, shots)
        mine = all_ref.at[pl.ds(2 * me, 2)]
        copies.append(send(mine, mine, ys.at[d - 1], yr.at[d - 1], (peer, sp)))
    for c in copies:
        c.wait()

    half = me // 2
    odd = lax.rem(me, 2)
    base = 4 * half
    p0 = all_ref[pair_ref[base + 2 * odd]]
    p1 = all_ref[pair_ref[base + 2 * odd + 1]]
    xx = all_ref[pair_ref[base + 2 + odd]]
    q0 = all_ref[pair_ref[base]]
    q1 = all_ref[pair_ref[base + 1]]
    sk = sk_ref[...]
    m_ref[0:64, :] = nt(p0, jnp.concatenate([p0, sk], axis=0))
    m_ref[64:128, :] = nt(p1, jnp.concatenate([p1, sk], axis=0))
    m_ref[128:192, :] = nt(xx, jnp.concatenate([q0, q1], axis=0))
    m_ref[192:256, :] = jnp.concatenate([nt(p0, p1), nt(p1, p0)], axis=1)

    copies = []
    for d in range(1, owners):
        peer = lax.rem(o + d, owners)
        copies.append(
            send(
                m_ref.at[pl.ds(pl.multiple_of(peer * rows, rows), rows)],
                rs.at[o], rss.at[d - 1], rsr.at[d - 1], (me, z * owners + peer),
            )
        )
    rs[o] = m_ref[pl.ds(pl.multiple_of(o * rows, rows), rows), :]
    for c in copies:
        c.wait()
    total = rs[0]
    for k in range(1, owners):
        total = total + rs[k]
    red[...] = total
    copies = []
    for d in range(1, depth):
        peer = lax.rem(z + d, depth) * owners + o
        copies.append(send(red, zb.at[z], zs.at[d - 1], zr.at[d - 1], (me, peer)))
    zb[z] = total
    for c in copies:
        c.wait()
    total = zb[0]
    for k in range(1, depth):
        total = total + zb[k]
    fin[...] = total
    copies = []
    for d in range(1, group):
        peer = lax.rem(line + d, group)
        target = (peer // owners, z * owners + lax.rem(peer, owners))
        copies.append(send(fin, g_ref.at[line], gs.at[d - 1], gr.at[d - 1], target))
    g_ref[line] = total
    for c in copies:
        c.wait()


def eliminate(mats):
    sub = lax.broadcasted_iota(jnp.int32, (8, LANES), 0)
    width = 4
    for kb in range(0, RANK, width):
        v0, off = kb // 8, kb % 8
        for w in mats:
            cols = [
                [jnp.broadcast_to(w[v][:, kb + j : kb + j + 1], (8, LANES)) for v in range(8)]
                for j in range(width)
            ]
            r = [jnp.broadcast_to(w[v0][off + i : off + i + 1, :], (8, LANES)) for i in range(width)]
            e = [
                [jnp.broadcast_to(cols[j][v0][off + i : off + i + 1, :], (8, LANES)) for j in range(width)]
                for i in range(width)
            ]
            for i in range(width):
                inv = 1.0 / e[i][i]
                r[i] = r[i] * inv
                for j in range(i + 1, width):
                    e[i][j] = e[i][j] * inv
                for k in range(width):
                    if k != i:
                        f = e[k][i]
                        r[k] = r[k] - f * r[i]
                        for j in range(i + 1, width):
                            e[k][j] = e[k][j] - f * e[i][j]
            for v in range(8):
                new = w[v]
                for j in range(width):
                    new = new - cols[j][v] * r[j]
                if v == v0:
                    for i in range(width):
                        new = jnp.where(sub == off + i, r[i], new)
                w[v] = new


def solve_all(mats):
    row = lax.broadcasted_iota(jnp.int32, (RANK, LANES), 0)
    lane = lax.broadcasted_iota(jnp.int32, (RANK, LANES), 1)
    diagonal = row == lane
    work = []
    for w in mats:
        trace = jnp.sum(jnp.where(diagonal, w, 0.0))
        ridge = 0.01 * trace / RANK + 1e-06
        w = jnp.where(diagonal, w + ridge, w)
        work.append([w[8 * v : 8 * v + 8] for v in range(8)])
    eliminate(work)
    out = []
    for w in work:
        full = jnp.concatenate(w, axis=0)
        full = full.astype(BF16).astype(F32)
        out.append(jnp.transpose(full)[RANK:])
    return out


def tree_kernel(scaling, all_ref, g_ref, pair_ref, out_ref, u_ref):
    me = lax.axis_index("shots")
    twice = scaling * scaling
    eights = [g_ref[p // 2, 64 * (p % 2) : 64 * (p % 2) + 64, :] for p in range(8)]
    first = solve_all(eights)
    second_in, pair_cols, crosses = [], [], []
    for m in range(4):
        c = jnp.concatenate([first[2 * m], first[2 * m + 1]], axis=1)
        a0, a1 = eights[2 * m], eights[2 * m + 1]
        mix = g_ref[m, 192:256, :]
        h = jnp.concatenate(
            [
                jnp.concatenate([a0[:, :RANK], mix[:, :RANK]], axis=1),
                jnp.concatenate([mix[:, RANK:], a1[:, :RANK]], axis=1),
            ],
            axis=0,
        )
        x = jnp.concatenate([a0[:, RANK:], a1[:, RANK:]], axis=0)
        gm = nt(nt(c, h, HI), c, HI)
        xm = jnp.dot(c, x, precision=HI, preferred_element_type=F32)
        second_in.append(jnp.concatenate([twice * gm, scaling * xm], axis=1))
        pair_cols.append(c)
    second = solve_all(second_in)
    third_in, quad_cols = [], []
    for h in range(2):
        d = jnp.concatenate([second[2 * h], second[2 * h + 1]], axis=1)
        c0, c1 = pair_cols[2 * h], pair_cols[2 * h + 1]
        k = jnp.concatenate([g_ref[2 * h, 128:192, :], g_ref[2 * h + 1, 128:192, :]], axis=0)
        g01 = twice * nt(nt(c0, k, HI), c1, HI)
        g10 = twice * nt(jnp.dot(c1, k, precision=HI, preferred_element_type=F32), c0, HI)
        b0, b1 = second_in[2 * h], second_in[2 * h + 1]
        hm = jnp.concatenate(
            [
                jnp.concatenate([b0[:, :RANK], g01], axis=1),
                jnp.concatenate([g10, b1[:, :RANK]], axis=1),
            ],
            axis=0,
        )
        x = jnp.concatenate([b0[:, RANK:], b1[:, RANK:]], axis=0)
        gm = nt(nt(d, hm, HI), d, HI)
        xm = jnp.dot(d, x, precision=HI, preferred_element_type=F32)
        third_in.append(jnp.concatenate([twice * gm, scaling * xm], axis=1))
        e0 = jnp.dot(second[2 * h], c0, precision=HI, preferred_element_type=F32)
        e1 = jnp.dot(second[2 * h + 1], c1, precision=HI, preferred_element_type=F32)
        quad_cols.append(jnp.concatenate([e0, e1], axis=1) * twice)
    third = solve_all(third_in)
    parts = [
        jnp.dot(third[h], quad_cols[h], precision=HI, preferred_element_type=F32) * scaling
        for h in range(2)
    ]
    u_ref[...] = jnp.concatenate(parts, axis=1)
    count = out_ref.shape[1]
    u = u_ref[pl.ds(pl.multiple_of(me * count, count), count), :].astype(BF16)
    total = None
    for p in range(8):
        term = jnp.dot(
            u[:, RANK * p : RANK * p + RANK], all_ref[pair_ref[p]], preferred_element_type=F32
        )
        total = term if total is None else total + term
    for x in range(out_ref.shape[0]):
        out_ref[x] = total[:, RANK * x : RANK * x + RANK].astype(BF16)


def body(depth, probes, sources, sketch, pairing):
    groups, rank, steps, fine_x, fine_y, fine_z = probes.shape
    shots = lax.axis_size("shots")
    space = lax.axis_size("space")
    owners = space // depth
    wxy, wz = weight_tables(fine_x, fine_y, fine_z)
    fine_xy = fine_x * fine_y
    chunk = 16
    vmem = pl.BlockSpec(memory_space=pltpu.VMEM)
    smem = pl.BlockSpec(memory_space=pltpu.SMEM)
    own, up, down = pl.pallas_call(
        restrict_kernel,
        grid=(groups, rank // chunk),
        in_specs=[
            pl.BlockSpec((1, chunk, steps, fine_xy, fine_z), lambda g, a: (g, a, 0, 0, 0)),
            pl.BlockSpec((1, steps, fine_xy, fine_z), lambda g, a: (g, 0, 0, 0)),
            pl.BlockSpec(wxy.shape, lambda g, a: (0, 0)),
            pl.BlockSpec(wz.shape, lambda g, a: (0, 0)),
        ],
        out_specs=[
            pl.BlockSpec((1, rank, 256), lambda g, a: (g, 0, 0)),
            pl.BlockSpec((1, rank, LANES), lambda g, a: (g, 0, 0)),
            pl.BlockSpec((1, rank, LANES), lambda g, a: (g, 0, 0)),
        ],
        out_shape=[
            jax.ShapeDtypeStruct((groups, rank, 256), F32),
            jax.ShapeDtypeStruct((groups, rank, LANES), BF16),
            jax.ShapeDtypeStruct((groups, rank, LANES), BF16),
        ],
        scratch_shapes=[pltpu.VMEM((rank * 16, LANES), F32)],
        name="restrict",
    )(
        probes.reshape(groups, rank, steps, fine_xy, fine_z),
        sources.reshape(groups, steps, fine_xy, fine_z),
        jnp.asarray(wxy),
        jnp.asarray(wz),
    )
    sk = jnp.transpose(sketch, (1, 0, 2)).reshape(rank, 256)
    rows = 256 // owners
    group = shots * owners
    dma = pltpu.SemaphoreType.DMA
    leaves, grams = pl.pallas_call(
        functools.partial(exchange_kernel, shots, depth, owners),
        in_specs=[vmem, vmem, vmem, vmem, smem],
        out_specs=[vmem, vmem],
        out_shape=[
            jax.ShapeDtypeStruct((groups * shots, rank, 256), BF16),
            jax.ShapeDtypeStruct((group, rows, LANES), F32),
        ],
        scratch_shapes=[
            pltpu.VMEM((2, groups, rank, LANES), BF16),
            pltpu.VMEM((256, LANES), F32),
            pltpu.VMEM((owners, rows, LANES), F32),
            pltpu.VMEM((rows, LANES), F32),
            pltpu.VMEM((depth, rows, LANES), F32),
            pltpu.VMEM((rows, LANES), F32),
            dma((2,)), dma((2,)),
            dma((shots - 1,)), dma((shots - 1,)),
            dma((owners - 1,)), dma((owners - 1,)),
            dma((depth - 1,)), dma((depth - 1,)),
            dma((group - 1,)), dma((group - 1,)),
        ],
        compiler_params=pltpu.CompilerParams(collective_id=0, has_side_effects=True),
        name="exchange",
    )(own, up, down, sk, pairing)
    scaling = math.sqrt(fine_x // 4 * space * 64 / rank)
    return pl.pallas_call(
        functools.partial(tree_kernel, scaling),
        in_specs=[vmem, vmem, smem],
        out_specs=vmem,
        out_shape=jax.ShapeDtypeStruct((fine_x // 4, rank // shots, 64), BF16),
        scratch_shapes=[pltpu.VMEM((rank, groups * shots * rank), F32)],
        name="tree",
    )(leaves, grams.reshape(shots, 256, LANES), pairing)


def solution(mesh):
    in_specs = (
        P("shots", None, None, "space", None, None),
        P("shots", None, "space", None, None),
        P("space", None, None),
        P(),
    )
    out_specs = P("space", "shots", None)
    depth = 8 if mesh.shape["space"] == 64 else 2
    return jax.shard_map(
        functools.partial(body, depth),
        mesh=mesh, in_specs=in_specs, out_specs=out_specs, check_vma=False,
    )
```

```python
import functools
import math

import jax
import jax.numpy as jnp
import numpy as np
from jax import lax
from jax.experimental import pallas as pl
from jax.experimental.pallas import tpu as pltpu
from jax.sharding import PartitionSpec as P

MESH = pl.DeviceIdType.MESH
F32 = jnp.float32
BF16 = jnp.bfloat16
HI = lax.Precision.HIGHEST
RANK = 64
LANES = 128


def spline_weight(distance):
    s = np.abs(distance / 4.0)
    inner = 2.0 / 3.0 - s**2 + 0.5 * s**3
    outer = np.maximum(2.0 - s, 0.0) ** 3 / 6.0
    return np.where(s < 1.0, inner, outer) / 4.0


def weight_tables(fine_x, fine_y, fine_z):
    coarse_x, coarse_y, coarse_z = fine_x // 4 + 4, fine_y // 4, fine_z // 4
    jx, jy, jz = np.arange(fine_x), np.arange(fine_y), np.arange(fine_z)
    ix, iy, iz = np.arange(coarse_x) - 2, np.arange(coarse_y), np.arange(coarse_z)
    wx = spline_weight(jx[None, :] + 0.5 - 4 * ix[:, None] - 2)
    wy = spline_weight(jy[None, :] + 0.5 - 4 * iy[:, None] - 2)
    wz = spline_weight(jz[:, None] + 0.5 - 4 * iz[None, :] - 2)
    wxy = np.einsum("ij,de->idje", wx, wy).reshape(coarse_x * coarse_y, fine_x * fine_y)
    wxy = np.concatenate([wxy, wxy], axis=1).astype(np.float32)
    high = wxy.astype(BF16)
    low = (wxy - high.astype(np.float32)).astype(BF16)
    side = 8
    block = np.zeros((side, fine_z, side, coarse_z), np.float32)
    for i in range(side):
        block[i, :, i, :] = wz
    block = block.reshape(side * fine_z, side * coarse_z).astype(BF16)
    return np.concatenate([high, low], axis=0), block


def nt(a, b, precision=None):
    return lax.dot_general(
        a, b, (((1,), (1,)), ((), ())), precision=precision, preferred_element_type=F32
    )


def nn(a, b, precision=None):
    return jnp.dot(a, b, precision=precision, preferred_element_type=F32)


def from_row(x, i):
    return jnp.take_along_axis(x, jnp.full((8, LANES), i, jnp.int32), axis=0)


def eliminate(mats, width):
    sub = lax.broadcasted_iota(jnp.int32, (8, LANES), 0)
    for kb in range(0, RANK, width):
        v0, off = kb // 8, kb % 8
        for w in mats:
            cols = [
                [jnp.broadcast_to(w[v][:, kb + j : kb + j + 1], (8, LANES)) for v in range(8)]
                for j in range(width)
            ]
            r = [from_row(w[v0], off + i) for i in range(width)]
            e = [[from_row(cols[j][v0], off + i) for j in range(width)] for i in range(width)]
            for i in range(width):
                inv = 1.0 / e[i][i]
                r[i] = r[i] * inv
                for j in range(i + 1, width):
                    e[i][j] = e[i][j] * inv
                for k in range(width):
                    if k != i:
                        f = e[k][i]
                        r[k] = r[k] - f * r[i]
                        for j in range(i + 1, width):
                            e[k][j] = e[k][j] - f * e[i][j]
            for v in range(8):
                new = w[v]
                for j in range(width):
                    new = new - cols[j][v] * r[j]
                if v == v0:
                    for i in range(width):
                        new = jnp.where(sub == off + i, r[i], new)
                w[v] = new


def solve_all(mats, width=4):
    row = lax.broadcasted_iota(jnp.int32, (RANK, LANES), 0)
    lane = lax.broadcasted_iota(jnp.int32, (RANK, LANES), 1)
    diagonal = row == lane
    work = []
    for w in mats:
        trace = jnp.sum(jnp.where(diagonal, w, 0.0), axis=(0, 1), keepdims=True)
        ridge = 0.01 * trace / RANK + 1e-06
        w = jnp.where(diagonal, w + ridge, w)
        work.append([w[8 * v : 8 * v + 8] for v in range(8)])
    eliminate(work, width)
    out = []
    for w in work:
        full = jnp.concatenate(w, axis=0)
        full = full.astype(BF16).astype(F32)
        out.append(jnp.transpose(full)[RANK:])
    return out


def two_by_two(a, b, c, d):
    return jnp.concatenate(
        [jnp.concatenate([a, b], axis=1), jnp.concatenate([c, d], axis=1)], axis=0
    )


def kernel(
    scaling, shots, depth, owners,
    p_ref, s_ref, wxy_ref, wz_ref, sk_ref, pair_ref,
    out_ref,
    t_ref, own, hsend, hrecv, leaf, skt,
    m_ref, rs, red, zb, fin, ga, us, ur, u_ref,
    hs, hr, ys, yr, rss, rsr, zs, zr, gs, gr, uss, usr,
):
    group_at = pl.program_id(0)
    step = pl.program_id(1)
    chunk = p_ref.shape[1]
    last_step = pl.num_programs(1) - 1
    me = lax.axis_index("shots")
    sp = lax.axis_index("space")
    count = depth * owners
    z = sp // owners
    o = lax.rem(sp, owners)
    right = lax.rem(sp + 1, count)
    left = lax.rem(sp + count - 1, count)
    half = me // 2
    odd = lax.rem(me, 2)
    base = 4 * half
    group = 2 * owners
    line = odd * owners + o
    rows = LANES // owners
    twice = scaling * scaling

    def owner_peer(d):
        return (me, z * owners + lax.rem(o + d, owners))

    def depth_peer(d):
        return (me, lax.rem(z + d, depth) * owners + o)

    def shot_peer(d):
        return (lax.rem(me + d, shots), sp)

    def group_peer(d):
        peer = lax.rem(line + d, group)
        return (2 * half + peer // owners, z * owners + lax.rem(peer, owners))

    barrier = pltpu.get_barrier_semaphore()

    @pl.when(jnp.logical_and(group_at == 0, step == 0))
    def _():
        targets = [(me, left), (me, right)]
        targets += [depth_peer(d) for d in range(1, depth)]
        targets += [shot_peer(d) for d in range(1, shots)]
        targets += [group_peer(d) for d in range(1, group)]
        for target in targets:
            pl.semaphore_signal(barrier, inc=1, device_id=target, device_id_type=MESH)
        skt[...] = jnp.concatenate([sk_ref[x] for x in range(sk_ref.shape[0])], axis=1)

    def remote(src, dst, ssem, rsem, target):
        return pltpu.make_async_remote_copy(
            src_ref=src, dst_ref=dst, send_sem=ssem, recv_sem=rsem,
            device_id=target, device_id_type=MESH,
        )

    def halo_copies(g):
        return [
            remote(hsend.at[g, 0], hrecv.at[g, 0], hs.at[g, 0], hr.at[g, 0], (me, right)),
            remote(hsend.at[g, 1], hrecv.at[g, 1], hs.at[g, 1], hr.at[g, 1], (me, left)),
        ]

    def leaf_copies(g):
        mine = leaf.at[2 * me + g]
        return [
            remote(mine, mine, ys.at[g, d - 1], yr.at[g, d - 1], shot_peer(d))
            for d in range(1, shots)
        ]

    src = s_ref[0].reshape(256, LANES)
    wxy = wxy_ref[...]
    for a in range(0, chunk, 2):
        first = p_ref[0, a].reshape(256, LANES) * src
        other = p_ref[0, a + 1].reshape(256, LANES) * src
        both = nn(wxy, jnp.concatenate([first, other], axis=1))
        both = both[:16] + both[16:]
        row = pl.multiple_of((step * chunk + a) * 16, 32)
        t_ref[pl.ds(row, 16), :] = both[:, :LANES]
        t_ref[pl.ds(row + 16, 16), :] = both[:, LANES:]

    def finish_group(g):
        wz = wz_ref[...]
        for part in range(2):
            cols = [t_ref[pl.ds(part * 8 + k, RANK, stride=16), :] for k in range(8)]
            y = nn(jnp.concatenate([q.astype(BF16) for q in cols], axis=1), wz)
            if part == 0:
                hsend[g, 1] = y[:, :LANES].astype(BF16)
                own[g, :, :LANES] = y[:, LANES:]
            else:
                own[g, :, LANES:] = y[:, :LANES]
                hsend[g, 0] = y[:, LANES:].astype(BF16)

    def make_leaf(g):
        below = jnp.where(sp > 0, hrecv[g, 0].astype(F32), 0.0)
        above = jnp.where(sp < count - 1, hrecv[g, 1].astype(F32), 0.0)
        lead = (own[g, :, :LANES] + below).astype(BF16)
        tail = (own[g, :, LANES:] + above).astype(BF16)
        leaf[2 * me + g, :, :LANES] = lead
        leaf[2 * me + g, :, LANES:] = tail

    @pl.when(jnp.logical_and(group_at == 0, step == last_step))
    def _():
        finish_group(0)
        pl.semaphore_wait(barrier, 2 + depth - 1 + shots - 1 + group - 1)
        for c in halo_copies(0):
            c.start()

    @pl.when(jnp.logical_and(group_at == 1, step == last_step))
    def _():
        finish_group(1)
        for c in halo_copies(1):
            c.start()
        for c in halo_copies(0):
            c.wait()
        make_leaf(0)
        for c in leaf_copies(0):
            c.start()
        for c in halo_copies(1):
            c.wait()
        make_leaf(1)
        for c in leaf_copies(1):
            c.start()
        for g in range(2):
            for c in leaf_copies(g):
                c.wait()

        p0 = leaf[pair_ref[base + 2 * odd]]
        p1 = leaf[pair_ref[base + 2 * odd + 1]]
        sk = skt[...]

        def scatter(part):
            out = []
            for d in range(1, owners):
                peer = lax.rem(o + d, owners)
                src_rows = m_ref.at[part, pl.ds(pl.multiple_of(peer * rows, rows), rows)]
                out.append(
                    remote(
                        src_rows, rs.at[part, o], rss.at[part, d - 1], rsr.at[part, d - 1],
                        owner_peer(d),
                    )
                )
            for c in out:
                c.start()
            rs[part, o] = m_ref[part, pl.ds(pl.multiple_of(o * rows, rows), rows), :]
            return out

        def along(part, copies):
            for c in copies:
                c.wait()
            total = rs[part, 0]
            for k in range(1, owners):
                total = total + rs[part, k]
            red[part] = total
            out = [
                remote(
                    red.at[part], zb.at[part, z], zs.at[part, d - 1], zr.at[part, d - 1],
                    depth_peer(d),
                )
                for d in range(1, depth)
            ]
            for c in out:
                c.start()
            zb[part, z] = total
            return out

        def spread(part, copies):
            for c in copies:
                c.wait()
            total = zb[part, 0]
            for k in range(1, depth):
                total = total + zb[part, k]
            fin[part] = total
            out = [
                remote(
                    fin.at[part], ga.at[part, line], gs.at[part, d - 1], gr.at[part, d - 1],
                    group_peer(d),
                )
                for d in range(1, group)
            ]
            for c in out:
                c.start()
            ga[part, line] = total
            return out

        m_ref[0, 0:64, :] = nt(p0, jnp.concatenate([p0, sk], axis=0))
        m_ref[0, 64:128, :] = nt(p1, jnp.concatenate([p1, sk], axis=0))
        first = scatter(0)
        xx = leaf[pair_ref[base + 2 + odd]]
        q0 = leaf[pair_ref[base]]
        q1 = leaf[pair_ref[base + 1]]
        m_ref[1, 0:64, :] = nt(xx, jnp.concatenate([q0, q1], axis=0))
        m_ref[1, 64:128, :] = jnp.concatenate([nt(p0, p1), nt(p1, p0)], axis=1)
        other = scatter(1)
        first = along(0, first)
        other = along(1, other)
        first = spread(0, first)
        other = spread(1, other)
        for c in first:
            c.wait()
        per = RANK // rows

        def block(part, index):
            return jnp.concatenate([ga[part, index * per + k] for k in range(per)], axis=0)

        aug = [block(0, p) for p in range(4)]
        c = solve_all(aug)
        for cp in other:
            cp.wait()
        pair_cols, second_in = [], []
        for m in range(2):
            cc = jnp.concatenate([c[2 * m], c[2 * m + 1]], axis=1)
            a0, a1 = aug[2 * m], aug[2 * m + 1]
            mix = block(1, 2 * m + 1)
            h = two_by_two(a0[:, :RANK], mix[:, :RANK], mix[:, RANK:], a1[:, :RANK])
            x = jnp.concatenate([a0[:, RANK:], a1[:, RANK:]], axis=0)
            gm = nt(nt(cc, h, HI), cc, HI)
            xm = nn(cc, x, HI)
            second_in.append(jnp.concatenate([twice * gm, scaling * xm], axis=1))
            pair_cols.append(cc)
        k = jnp.concatenate([block(1, 0), block(1, 2)], axis=0)
        g01 = twice * nt(nt(pair_cols[0], k, HI), pair_cols[1], HI)
        g10 = twice * nt(nn(pair_cols[1], k, HI), pair_cols[0], HI)
        d = solve_all(second_in)
        dd = jnp.concatenate(d, axis=1)
        b0, b1 = second_in
        hm = two_by_two(b0[:, :RANK], g01, g10, b1[:, :RANK])
        x = jnp.concatenate([b0[:, RANK:], b1[:, RANK:]], axis=0)
        gm = nt(nt(dd, hm, HI), dd, HI)
        xm = nn(dd, x, HI)
        quad = twice * jnp.concatenate([nn(d[m], pair_cols[m], HI) for m in range(2)], axis=1)
        third = solve_all([jnp.concatenate([twice * gm, scaling * xm], axis=1)], 8)
        u_ref[...] = scaling * nn(third[0], quad, HI)
        width = out_ref.shape[1]
        partner = shots - 1 - me
        us[...] = u_ref[pl.ds(pl.multiple_of(partner * width, width), width), :].astype(BF16)
        trade = remote(us, ur, uss, usr, (partner, sp))
        trade.start()
        u = u_ref[pl.ds(pl.multiple_of(me * width, width), width), :].astype(BF16)
        total = None
        for p in range(4):
            term = nn(u[:, RANK * p : RANK * p + RANK], leaf[pair_ref[base + p]])
            total = term if total is None else total + term
        trade.wait()
        v = ur[...]
        for p in range(4):
            total = total + nn(v[:, RANK * p : RANK * p + RANK], leaf[pair_ref[4 - base + p]])
        for i in range(out_ref.shape[0]):
            out_ref[i] = total[:, RANK * i : RANK * i + RANK].astype(BF16)


def body(depth, probes, sources, sketch, pairing):
    groups, rank, steps, fine_x, fine_y, fine_z = probes.shape
    shots = lax.axis_size("shots")
    space = lax.axis_size("space")
    owners = space // depth
    wxy, wz = weight_tables(fine_x, fine_y, fine_z)
    fine_xy = fine_x * fine_y
    chunk = 16
    rows = LANES // owners
    group = 2 * owners
    dma = pltpu.SemaphoreType.DMA
    vmem = pltpu.VMEM
    scaling = math.sqrt(fine_x // 4 * space * 64 / rank)
    out_shape = (fine_x // 4, rank // shots, 64)
    return pl.pallas_call(
        functools.partial(kernel, scaling, shots, depth, owners),
        grid=(groups, rank // chunk),
        in_specs=[
            pl.BlockSpec((1, chunk, steps, fine_xy, fine_z), lambda g, a: (g, a, 0, 0, 0)),
            pl.BlockSpec((1, steps, fine_xy, fine_z), lambda g, a: (g, 0, 0, 0)),
            pl.BlockSpec(wxy.shape, lambda g, a: (0, 0)),
            pl.BlockSpec(wz.shape, lambda g, a: (0, 0)),
            pl.BlockSpec(sketch.shape, lambda g, a: (0, 0, 0)),
            pl.BlockSpec(memory_space=pltpu.SMEM),
        ],
        out_specs=pl.BlockSpec(out_shape, lambda g, a: (0, 0, 0)),
        out_shape=jax.ShapeDtypeStruct(out_shape, BF16),
        scratch_shapes=[
            vmem((rank * 16, LANES), F32),
            vmem((groups, rank, 256), F32),
            vmem((groups, 2, rank, LANES), BF16),
            vmem((groups, 2, rank, LANES), BF16),
            vmem((groups * shots, rank, 256), BF16),
            vmem((rank, 256), BF16),
            vmem((2, LANES, LANES), F32),
            vmem((2, owners, rows, LANES), F32),
            vmem((2, rows, LANES), F32),
            vmem((2, depth, rows, LANES), F32),
            vmem((2, rows, LANES), F32),
            vmem((2, group, rows, LANES), F32),
            vmem((rank // shots, 256), BF16),
            vmem((rank // shots, 256), BF16),
            vmem((rank, 256), F32),
            dma((groups, 2)), dma((groups, 2)),
            dma((groups, shots - 1)), dma((groups, shots - 1)),
            dma((2, owners - 1)), dma((2, owners - 1)),
            dma((2, depth - 1)), dma((2, depth - 1)),
            dma((2, group - 1)), dma((2, group - 1)),
            dma, dma,
        ],
        compiler_params=pltpu.CompilerParams(collective_id=0, has_side_effects=True),
        name="merge",
    )(
        probes.reshape(groups, rank, steps, fine_xy, fine_z),
        sources.reshape(groups, steps, fine_xy, fine_z),
        jnp.asarray(wxy),
        jnp.asarray(wz),
        sketch,
        pairing,
    )


def solution(mesh):
    in_specs = (
        P("shots", None, None, "space", None, None),
        P("shots", None, "space", None, None),
        P("space", None, None),
        P(),
    )
    out_specs = P("space", "shots", None)
    depth = 8 if mesh.shape["space"] == 64 else 2
    return jax.shard_map(
        functools.partial(body, depth),
        mesh=mesh, in_specs=in_specs, out_specs=out_specs, check_vma=False,
    )
```

```python
import functools
import math

import jax
import jax.numpy as jnp
import numpy as np
from jax import lax
from jax.experimental import pallas as pl
from jax.experimental.pallas import tpu as pltpu
from jax.sharding import PartitionSpec as P

MESH = pl.DeviceIdType.MESH
F32 = jnp.float32
BF16 = jnp.bfloat16
RANK = 64
LANES = 128


def spline_weight(distance):
    s = np.abs(distance / 4.0)
    inner = 2.0 / 3.0 - s**2 + 0.5 * s**3
    outer = np.maximum(2.0 - s, 0.0) ** 3 / 6.0
    return np.where(s < 1.0, inner, outer) / 4.0


def weight_tables(fine_x, fine_y, fine_z):
    coarse_x, coarse_y, coarse_z = fine_x // 4 + 4, fine_y // 4, fine_z // 4
    jx, jy, jz = np.arange(fine_x), np.arange(fine_y), np.arange(fine_z)
    ix, iy, iz = np.arange(coarse_x) - 2, np.arange(coarse_y), np.arange(coarse_z)
    wx = spline_weight(jx[None, :] + 0.5 - 4 * ix[:, None] - 2)
    wy = spline_weight(jy[None, :] + 0.5 - 4 * iy[:, None] - 2)
    wz = spline_weight(jz[:, None] + 0.5 - 4 * iz[None, :] - 2)
    wxy = np.einsum("ij,de->idje", wx, wy).reshape(coarse_x * coarse_y, fine_x * fine_y)
    wxy = np.concatenate([wxy, wxy], axis=1).astype(np.float32)
    high = wxy.astype(BF16)
    low = (wxy - high.astype(np.float32)).astype(BF16)
    side = 8
    block = np.zeros((side, fine_z, side, coarse_z), np.float32)
    for i in range(side):
        block[i, :, i, :] = wz
    block = block.reshape(side * fine_z, side * coarse_z).astype(BF16)
    return np.concatenate([high, low], axis=0), block


def nt(a, b):
    return lax.dot_general(
        a, b, (((1,), (1,)), ((), ())), preferred_element_type=F32
    )


def nn(a, b):
    return jnp.dot(a, b, preferred_element_type=F32)


def from_row(x, i):
    return jnp.take_along_axis(x, jnp.full((8, LANES), i, jnp.int32), axis=0)


def eliminate(mats, width):
    sub = lax.broadcasted_iota(jnp.int32, (8, LANES), 0)
    for kb in range(0, RANK, width):
        v0, off = kb // 8, kb % 8
        for w in mats:
            cols = [
                [jnp.broadcast_to(w[v][:, kb + j : kb + j + 1], (8, LANES)) for v in range(8)]
                for j in range(width)
            ]
            r = [from_row(w[v0], off + i) for i in range(width)]
            e = [[from_row(cols[j][v0], off + i) for j in range(width)] for i in range(width)]
            for i in range(width):
                inv = 1.0 / e[i][i]
                r[i] = r[i] * inv
                for j in range(i + 1, width):
                    e[i][j] = e[i][j] * inv
                for k in range(width):
                    if k != i:
                        f = e[k][i]
                        r[k] = r[k] - f * r[i]
                        for j in range(i + 1, width):
                            e[k][j] = e[k][j] - f * e[i][j]
            for v in range(8):
                new = w[v]
                for j in range(width):
                    new = new - cols[j][v] * r[j]
                if v == v0:
                    for i in range(width):
                        new = jnp.where(sub == off + i, r[i], new)
                w[v] = new


def solve_all(mats, width=4):
    row = lax.broadcasted_iota(jnp.int32, (RANK, LANES), 0)
    lane = lax.broadcasted_iota(jnp.int32, (RANK, LANES), 1)
    diagonal = row == lane
    work = []
    for w in mats:
        trace = jnp.sum(jnp.where(diagonal, w, 0.0), axis=(0, 1), keepdims=True)
        ridge = 0.01 * trace / RANK + 1e-06
        w = jnp.where(diagonal, w + ridge, w)
        work.append([w[8 * v : 8 * v + 8] for v in range(8)])
    eliminate(work, width)
    out = []
    for w in work:
        full = jnp.concatenate(w, axis=0)
        out.append(jnp.transpose(full)[RANK:].astype(BF16))
    return out


def split(x, terms):
    out = []
    for _ in range(terms - 1):
        part = x.astype(BF16)
        out.append(part)
        x = x - part.astype(F32)
    out.append(x.astype(BF16))
    return out


def exact_nn(c, x, terms=3):
    return nn(jnp.concatenate([c] * terms, axis=1), jnp.concatenate(split(x, terms), axis=0))


def exact_nt(x, c, terms=3):
    return nt(jnp.concatenate(split(x, terms), axis=1), jnp.concatenate([c] * terms, axis=1))


def gram_and_cross(c, h, x, scaling):
    both = exact_nn(c, jnp.concatenate([h, x], axis=1))
    gm = exact_nt(both[:, :LANES], c)
    return jnp.concatenate([(scaling * scaling) * gm, scaling * both[:, LANES:]], axis=1)


def two_by_two(a, b, c, d):
    return jnp.concatenate(
        [jnp.concatenate([a, b], axis=1), jnp.concatenate([c, d], axis=1)], axis=0
    )


def kernel(
    scaling, shots, depth, owners,
    p_hbm, s_hbm, wxy_hbm, wz_hbm, sk_hbm, pair_ref,
    out_ref,
    p_ref, s_ref, wxy_ref, wz_ref, sk_ref, psem, csem,
    t_ref, own, hsend, hrecv, leaf, skt,
    m_ref, rs, red, zb, fin, ga, us, ur, u_ref,
    hs, hr, ys, yr, rss, rsr, zs, zr, gs, gr, uss, usr,
):
    chunk = 16
    blocks = RANK // chunk

    def load(g, i):
        at = pl.ds(i * chunk, chunk)
        return pltpu.make_async_copy(p_hbm.at[g, at], p_ref.at[g, at], psem.at[g, i])

    small = [
        pltpu.make_async_copy(src, dst, csem.at[i])
        for i, (src, dst) in enumerate(
            [(s_hbm, s_ref), (wxy_hbm, wxy_ref), (wz_hbm, wz_ref), (sk_hbm, sk_ref)]
        )
    ]
    small[0].start()
    small[1].start()
    for i in range(blocks):
        load(0, i).start()
    small[2].start()
    for i in range(blocks):
        load(1, i).start()
    small[3].start()
    me = lax.axis_index("shots")
    sp = lax.axis_index("space")
    count = depth * owners
    z = sp // owners
    o = lax.rem(sp, owners)
    right = lax.rem(sp + 1, count)
    left = lax.rem(sp + count - 1, count)
    half = me // 2
    odd = lax.rem(me, 2)
    base = 4 * half
    group = 2 * owners
    line = odd * owners + o
    rows = LANES // owners
    twice = scaling * scaling

    def owner_peer(d):
        return (me, z * owners + lax.rem(o + d, owners))

    def depth_peer(d):
        return (me, lax.rem(z + d, depth) * owners + o)

    def shot_peer(d):
        return (lax.rem(me + d, shots), sp)

    def group_peer(d):
        peer = lax.rem(line + d, group)
        return (2 * half + peer // owners, z * owners + lax.rem(peer, owners))

    barrier = pltpu.get_barrier_semaphore()

    targets = [(me, left), (me, right)]
    targets += [depth_peer(d) for d in range(1, depth)]
    targets += [shot_peer(d) for d in range(1, shots)]
    targets += [group_peer(d) for d in range(1, group)]
    for target in targets:
        pl.semaphore_signal(barrier, inc=1, device_id=target, device_id_type=MESH)

    def remote(src, dst, ssem, rsem, target):
        return pltpu.make_async_remote_copy(
            src_ref=src, dst_ref=dst, send_sem=ssem, recv_sem=rsem,
            device_id=target, device_id_type=MESH,
        )

    def halo_copies(g):
        return [
            remote(hsend.at[g, 0], hrecv.at[g, 0], hs.at[g, 0], hr.at[g, 0], (me, right)),
            remote(hsend.at[g, 1], hrecv.at[g, 1], hs.at[g, 1], hr.at[g, 1], (me, left)),
        ]

    def leaf_copies(g):
        mine = leaf.at[2 * me + g]
        return [
            remote(mine, mine, ys.at[g, d - 1], yr.at[g, d - 1], shot_peer(d))
            for d in range(1, shots)
        ]

    small[0].wait()
    small[1].wait()
    wxy = wxy_ref[...]

    def restrict_group(g):
        src = s_ref[g].reshape(256, LANES)

        def one(i, carry):
            load(g, i).wait()
            for a in range(0, chunk, 2):
                at = i * chunk + a
                first = p_ref[g, at].reshape(256, LANES) * src
                other = p_ref[g, at + 1].reshape(256, LANES) * src
                both = nn(wxy, jnp.concatenate([first, other], axis=1))
                both = both[:16] + both[16:]
                row = pl.multiple_of(at * 16, 32)
                t_ref[pl.ds(row, 16), :] = both[:, :LANES]
                t_ref[pl.ds(row + 16, 16), :] = both[:, LANES:]
            return carry

        lax.fori_loop(0, blocks, one, 0)

    def finish_group(g):
        wz = wz_ref[...]
        for part in range(2):
            cols = [t_ref[pl.ds(part * 8 + k, RANK, stride=16), :] for k in range(8)]
            y = nn(jnp.concatenate([q.astype(BF16) for q in cols], axis=1), wz)
            if part == 0:
                hsend[g, 1] = y[:, :LANES].astype(BF16)
                own[g, :, :LANES] = y[:, LANES:]
            else:
                own[g, :, LANES:] = y[:, :LANES]
                hsend[g, 0] = y[:, LANES:].astype(BF16)

    def make_leaf(g):
        below = jnp.where(sp > 0, hrecv[g, 0].astype(F32), 0.0)
        above = jnp.where(sp < count - 1, hrecv[g, 1].astype(F32), 0.0)
        lead = (own[g, :, :LANES] + below).astype(BF16)
        tail = (own[g, :, LANES:] + above).astype(BF16)
        leaf[2 * me + g, :, :LANES] = lead
        leaf[2 * me + g, :, LANES:] = tail

    restrict_group(0)
    small[2].wait()
    finish_group(0)
    pl.semaphore_wait(barrier, len(targets))
    for c in halo_copies(0):
        c.start()
    restrict_group(1)
    finish_group(1)
    for c in halo_copies(1):
        c.start()
    small[3].wait()
    skt[...] = jnp.concatenate([sk_ref[x] for x in range(sk_ref.shape[0])], axis=1)
    for c in halo_copies(0):
        c.wait()
    make_leaf(0)
    for c in leaf_copies(0):
        c.start()
    for c in halo_copies(1):
        c.wait()
    make_leaf(1)
    for c in leaf_copies(1):
        c.start()
    for g in range(2):
        for c in leaf_copies(g):
            c.wait()

    p0 = leaf[pair_ref[base + 2 * odd]]
    p1 = leaf[pair_ref[base + 2 * odd + 1]]
    sk = skt[...]

    def scatter(part):
        out = []
        for d in range(1, owners):
            peer = lax.rem(o + d, owners)
            src_rows = m_ref.at[part, pl.ds(pl.multiple_of(peer * rows, rows), rows)]
            out.append(
                remote(
                    src_rows, rs.at[part, o], rss.at[part, d - 1], rsr.at[part, d - 1],
                    owner_peer(d),
                )
            )
        for c in out:
            c.start()
        rs[part, o] = m_ref[part, pl.ds(pl.multiple_of(o * rows, rows), rows), :]
        return out

    def along(part, copies):
        for c in copies:
            c.wait()
        total = rs[part, 0]
        for k in range(1, owners):
            total = total + rs[part, k]
        red[part] = total
        out = [
            remote(
                red.at[part], zb.at[part, z], zs.at[part, d - 1], zr.at[part, d - 1],
                depth_peer(d),
            )
            for d in range(1, depth)
        ]
        for c in out:
            c.start()
        zb[part, z] = total
        return out

    def spread(part, copies):
        for c in copies:
            c.wait()
        total = zb[part, 0]
        for k in range(1, depth):
            total = total + zb[part, k]
        fin[part] = total
        out = [
            remote(
                fin.at[part], ga.at[part, line], gs.at[part, d - 1], gr.at[part, d - 1],
                group_peer(d),
            )
            for d in range(1, group)
        ]
        for c in out:
            c.start()
        ga[part, line] = total
        return out

    m_ref[0, 0:64, :] = nt(p0, jnp.concatenate([p0, sk], axis=0))
    m_ref[0, 64:128, :] = nt(p1, jnp.concatenate([p1, sk], axis=0))
    first = scatter(0)
    xx = leaf[pair_ref[base + 2 + odd]]
    q0 = leaf[pair_ref[base]]
    q1 = leaf[pair_ref[base + 1]]
    m_ref[1, 0:64, :] = nt(xx, jnp.concatenate([q0, q1], axis=0))
    m_ref[1, 64:128, :] = jnp.concatenate([nt(p0, p1), nt(p1, p0)], axis=1)
    other = scatter(1)
    first = along(0, first)
    other = along(1, other)
    first = spread(0, first)
    other = spread(1, other)
    for c in first:
        c.wait()
    per = RANK // rows

    def block(part, index):
        return jnp.concatenate([ga[part, index * per + k] for k in range(per)], axis=0)

    aug = [block(0, p) for p in range(4)]
    c = solve_all(aug)
    for cp in other:
        cp.wait()
    pair_cols, second_in = [], []
    for m in range(2):
        cc = jnp.concatenate([c[2 * m], c[2 * m + 1]], axis=1)
        a0, a1 = aug[2 * m], aug[2 * m + 1]
        mix = block(1, 2 * m + 1)
        h = two_by_two(a0[:, :RANK], mix[:, :RANK], mix[:, RANK:], a1[:, :RANK])
        x = jnp.concatenate([a0[:, RANK:], a1[:, RANK:]], axis=0)
        second_in.append(gram_and_cross(cc, h, x, scaling))
        pair_cols.append(cc)
    k = jnp.concatenate([block(1, 0), block(1, 2)], axis=0)
    g10 = twice * exact_nt(exact_nn(pair_cols[1], k), pair_cols[0])
    g01 = jnp.transpose(g10)
    d = solve_all(second_in)
    dd = jnp.concatenate(d, axis=1)
    b0, b1 = second_in
    hm = two_by_two(b0[:, :RANK], g01, g10, b1[:, :RANK])
    x = jnp.concatenate([b0[:, RANK:], b1[:, RANK:]], axis=0)
    quad = twice * jnp.concatenate([nn(d[m], pair_cols[m]) for m in range(2)], axis=1)
    third = solve_all([gram_and_cross(dd, hm, x, scaling)], 8)
    u_ref[...] = scaling * exact_nn(third[0], quad, 2)
    width = out_ref.shape[1]
    partner = shots - 1 - me
    us[...] = u_ref[pl.ds(pl.multiple_of(partner * width, width), width), :].astype(BF16)
    trade = remote(us, ur, uss, usr, (partner, sp))
    trade.start()
    u = u_ref[pl.ds(pl.multiple_of(me * width, width), width), :].astype(BF16)
    total = None
    for p in range(4):
        term = nn(u[:, RANK * p : RANK * p + RANK], leaf[pair_ref[base + p]])
        total = term if total is None else total + term
    trade.wait()
    v = ur[...]
    for p in range(4):
        total = total + nn(v[:, RANK * p : RANK * p + RANK], leaf[pair_ref[4 - base + p]])
    for i in range(out_ref.shape[0]):
        out_ref[i] = total[:, RANK * i : RANK * i + RANK].astype(BF16)


def body(depth, probes, sources, sketch, pairing):
    groups, rank, steps, fine_x, fine_y, fine_z = probes.shape
    shots = lax.axis_size("shots")
    space = lax.axis_size("space")
    owners = space // depth
    wxy, wz = weight_tables(fine_x, fine_y, fine_z)
    fine_xy = fine_x * fine_y
    chunk = 16
    rows = LANES // owners
    group = 2 * owners
    dma = pltpu.SemaphoreType.DMA
    vmem = pltpu.VMEM
    scaling = math.sqrt(fine_x // 4 * space * 64 / rank)
    out_shape = (fine_x // 4, rank // shots, 64)
    return pl.pallas_call(
        functools.partial(kernel, scaling, shots, depth, owners),
        in_specs=[pl.BlockSpec(memory_space=pl.ANY)] * 5
        + [pl.BlockSpec(memory_space=pltpu.SMEM)],
        out_specs=pl.BlockSpec(memory_space=pltpu.VMEM),
        out_shape=jax.ShapeDtypeStruct(out_shape, BF16),
        scratch_shapes=[
            vmem((groups, rank, steps, fine_xy, fine_z), BF16),
            vmem((groups, steps, fine_xy, fine_z), BF16),
            vmem(wxy.shape, BF16),
            vmem(wz.shape, BF16),
            vmem(sketch.shape, BF16),
            dma((groups, rank // chunk)),
            dma((4,)),
            vmem((rank * 16, LANES), F32),
            vmem((groups, rank, 256), F32),
            vmem((groups, 2, rank, LANES), BF16),
            vmem((groups, 2, rank, LANES), BF16),
            vmem((groups * shots, rank, 256), BF16),
            vmem((rank, 256), BF16),
            vmem((2, LANES, LANES), F32),
            vmem((2, owners, rows, LANES), F32),
            vmem((2, rows, LANES), F32),
            vmem((2, depth, rows, LANES), F32),
            vmem((2, rows, LANES), F32),
            vmem((2, group, rows, LANES), F32),
            vmem((rank // shots, 256), BF16),
            vmem((rank // shots, 256), BF16),
            vmem((rank, 256), F32),
            dma((groups, 2)), dma((groups, 2)),
            dma((groups, shots - 1)), dma((groups, shots - 1)),
            dma((2, owners - 1)), dma((2, owners - 1)),
            dma((2, depth - 1)), dma((2, depth - 1)),
            dma((2, group - 1)), dma((2, group - 1)),
            dma, dma,
        ],
        compiler_params=pltpu.CompilerParams(collective_id=0, has_side_effects=True),
        name="merge",
    )(
        probes.reshape(groups, rank, steps, fine_xy, fine_z),
        sources.reshape(groups, steps, fine_xy, fine_z),
        jnp.asarray(wxy),
        jnp.asarray(wz),
        sketch,
        pairing,
    )


def solution(mesh):
    in_specs = (
        P("shots", None, None, "space", None, None),
        P("shots", None, "space", None, None),
        P("space", None, None),
        P(),
    )
    out_specs = P("space", "shots", None)
    depth = 8 if mesh.shape["space"] == 64 else 2
    return jax.shard_map(
        functools.partial(body, depth),
        mesh=mesh, in_specs=in_specs, out_specs=out_specs, check_vma=False,
    )
```

```python
import functools
import math

import jax
import jax.numpy as jnp
import numpy as np
from jax import lax
from jax.experimental import pallas as pl
from jax.experimental.pallas import tpu as pltpu
from jax.sharding import PartitionSpec as P

MESH = pl.DeviceIdType.MESH
F32 = jnp.float32
BF16 = jnp.bfloat16
RANK = 64
LANES = 128


def spline_weight(distance):
    s = np.abs(distance / 4.0)
    inner = 2.0 / 3.0 - s**2 + 0.5 * s**3
    outer = np.maximum(2.0 - s, 0.0) ** 3 / 6.0
    return np.where(s < 1.0, inner, outer) / 4.0


def weight_tables(fine_x, fine_y, fine_z):
    coarse_x, coarse_y, coarse_z = fine_x // 4 + 4, fine_y // 4, fine_z // 4
    jx, jy, jz = np.arange(fine_x), np.arange(fine_y), np.arange(fine_z)
    ix, iy, iz = np.arange(coarse_x) - 2, np.arange(coarse_y), np.arange(coarse_z)
    wx = spline_weight(jx[None, :] + 0.5 - 4 * ix[:, None] - 2)
    wy = spline_weight(jy[None, :] + 0.5 - 4 * iy[:, None] - 2)
    wz = spline_weight(jz[:, None] + 0.5 - 4 * iz[None, :] - 2)
    wxy = np.einsum("ij,de->idje", wx, wy).reshape(coarse_x * coarse_y, fine_x * fine_y)
    wxy = np.concatenate([wxy, wxy], axis=1).astype(np.float32)
    high = wxy.astype(BF16)
    low = (wxy - high.astype(np.float32)).astype(BF16)
    side = 8
    block = np.zeros((side, fine_z, side, coarse_z), np.float32)
    for i in range(side):
        block[i, :, i, :] = wz
    block = block.reshape(side * fine_z, side * coarse_z).astype(BF16)
    return np.concatenate([high, low], axis=0), block


def nt(a, b):
    return lax.dot_general(
        a, b, (((1,), (1,)), ((), ())), preferred_element_type=F32
    )


def nn(a, b):
    return jnp.dot(a, b, preferred_element_type=F32)


def from_row(x, i):
    return jnp.take_along_axis(x, jnp.full((8, LANES), i, jnp.int32), axis=0)


def eliminate(mats, width):
    sub = lax.broadcasted_iota(jnp.int32, (8, LANES), 0)
    for kb in range(0, RANK, width):
        v0, off = kb // 8, kb % 8
        for w in mats:
            cols = [
                [jnp.broadcast_to(w[v][:, kb + j : kb + j + 1], (8, LANES)) for v in range(8)]
                for j in range(width)
            ]
            r = [from_row(w[v0], off + i) for i in range(width)]
            e = [[from_row(cols[j][v0], off + i) for j in range(width)] for i in range(width)]
            for i in range(width):
                inv = 1.0 / e[i][i]
                r[i] = r[i] * inv
                for j in range(i + 1, width):
                    e[i][j] = e[i][j] * inv
                for k in range(width):
                    if k != i:
                        f = e[k][i]
                        r[k] = r[k] - f * r[i]
                        for j in range(i + 1, width):
                            e[k][j] = e[k][j] - f * e[i][j]
            for v in range(8):
                new = w[v]
                for j in range(width):
                    new = new - cols[j][v] * r[j]
                if v == v0:
                    for i in range(width):
                        new = jnp.where(sub == off + i, r[i], new)
                w[v] = new


def solve_all(mats, width=4):
    row = lax.broadcasted_iota(jnp.int32, (RANK, LANES), 0)
    lane = lax.broadcasted_iota(jnp.int32, (RANK, LANES), 1)
    diagonal = row == lane
    work = []
    for w in mats:
        trace = jnp.sum(jnp.where(diagonal, w, 0.0), axis=(0, 1), keepdims=True)
        ridge = 0.01 * trace / RANK + 1e-06
        w = jnp.where(diagonal, w + ridge, w)
        work.append([w[8 * v : 8 * v + 8] for v in range(8)])
    eliminate(work, width)
    out = []
    for w in work:
        full = jnp.concatenate(w, axis=0)
        out.append(jnp.transpose(full)[RANK:].astype(BF16))
    return out


def split(x, terms):
    out = []
    for _ in range(terms - 1):
        part = x.astype(BF16)
        out.append(part)
        x = x - part.astype(F32)
    out.append(x.astype(BF16))
    return out


def exact_nn(c, x, terms=3):
    return nn(jnp.concatenate([c] * terms, axis=1), jnp.concatenate(split(x, terms), axis=0))


def exact_nt(x, c, terms=3):
    return nt(jnp.concatenate(split(x, terms), axis=1), jnp.concatenate([c] * terms, axis=1))


def gram_and_cross(c, h, x, scaling):
    both = exact_nn(c, jnp.concatenate([h, x], axis=1))
    gm = exact_nt(both[:, :LANES], c)
    return jnp.concatenate([(scaling * scaling) * gm, scaling * both[:, LANES:]], axis=1)


def two_by_two(a, b, c, d):
    return jnp.concatenate(
        [jnp.concatenate([a, b], axis=1), jnp.concatenate([c, d], axis=1)], axis=0
    )


def kernel(
    scaling, shots, depth, owners,
    p_hbm, s_hbm, wxy_hbm, wz_hbm, sk_hbm, pair_ref,
    out_ref,
    p_ref, s_ref, wxy_ref, wz_ref, sk_ref, psem, csem,
    t_ref, part_of, hsend, hrecv, leaf, skt,
    m_ref, rs, red, zb, fin, ga, us, ur, u_ref,
    hs, hr, ys, yr, rss, rsr, zs, zr, gs, gr, uss, usr,
):
    chunk = 16
    blocks = RANK // chunk

    def load(g, i):
        at = pl.ds(i * chunk, chunk)
        return pltpu.make_async_copy(p_hbm.at[g, at], p_ref.at[g, at], psem.at[g, i])

    small = [
        pltpu.make_async_copy(src, dst, csem.at[i])
        for i, (src, dst) in enumerate(
            [(s_hbm, s_ref), (wxy_hbm, wxy_ref), (wz_hbm, wz_ref), (sk_hbm, sk_ref)]
        )
    ]
    small[0].start()
    small[1].start()
    for i in range(blocks):
        load(0, i).start()
    small[2].start()
    for i in range(blocks):
        load(1, i).start()
    small[3].start()
    me = lax.axis_index("shots")
    sp = lax.axis_index("space")
    count = depth * owners
    z = sp // owners
    o = lax.rem(sp, owners)
    right = lax.rem(sp + 1, count)
    left = lax.rem(sp + count - 1, count)
    half = me // 2
    odd = lax.rem(me, 2)
    base = 4 * half
    group = 2 * owners
    line = odd * owners + o
    rows = LANES // owners
    twice = scaling * scaling

    across = owners // 2
    at_x = o // 2
    core = lax.rem(o, 2)

    def ring(d, size):
        return min(d, size - d)

    def near(dx, dc):
        return lax.rem(at_x + dx, across) * 2 + lax.rem(core + dc, 2)

    group_offsets = sorted(
        [(dy, dx, dc) for dy in range(2) for dx in range(across) for dc in range(2)][1:],
        key=lambda d: (-d[0] - ring(d[1], across), -d[2]),
    )
    owner_offsets = [d for d in group_offsets if d[0] == 0]
    depth_offsets = sorted(range(1, depth), key=lambda d: -ring(d, depth))
    shot_offsets = sorted(range(shots), key=lambda d: -ring(d, shots))

    def slot(offset):
        dy, dx, dc = offset
        return dy * owners + dx * 2 + dc - 1

    def depth_peer(d):
        return (me, lax.rem(z + d, depth) * owners + o)

    def shot_peer(d):
        return (lax.rem(me + d, shots), sp)

    def group_peer(offset):
        dy, dx, dc = offset
        return (2 * half + lax.rem(odd + dy, 2), z * owners + near(dx, dc))

    barrier = pltpu.get_barrier_semaphore()

    targets = [(lax.rem(me + d, shots), side) for d in shot_offsets for side in (left, right)]
    targets += [depth_peer(d) for d in depth_offsets]
    targets += [shot_peer(d) for d in shot_offsets if d]
    targets += [group_peer(d) for d in group_offsets]
    for target in targets:
        pl.semaphore_signal(barrier, inc=1, device_id=target, device_id_type=MESH)

    def remote(src, dst, ssem, rsem, target):
        return pltpu.make_async_remote_copy(
            src_ref=src, dst_ref=dst, send_sem=ssem, recv_sem=rsem,
            device_id=target, device_id_type=MESH,
        )

    def piece_copies(g):
        mine = part_of.at[2 * me + g]
        out = []
        for d in shot_offsets:
            shot = lax.rem(me + d, shots)
            for side, peer in enumerate((right, left)):
                out.append(
                    remote(
                        hsend.at[g, side], hrecv.at[2 * me + g, side],
                        hs.at[g, side, d], hr.at[g, side, d], (shot, peer),
                    )
                )
            if d:
                out.append(remote(mine, mine, ys.at[g, d - 1], yr.at[g, d - 1], (shot, sp)))
        return out

    small[0].wait()
    small[1].wait()
    wxy = wxy_ref[...]

    def restrict_group(g):
        src = s_ref[g].reshape(256, LANES)

        def one(i, carry):
            load(g, i).wait()
            for a in range(0, chunk, 2):
                at = i * chunk + a
                first = p_ref[g, at].reshape(256, LANES) * src
                other = p_ref[g, at + 1].reshape(256, LANES) * src
                both = nn(wxy, jnp.concatenate([first, other], axis=1))
                both = both[:16] + both[16:]
                row = pl.multiple_of(at * 16, 32)
                t_ref[pl.ds(row, 16), :] = both[:, :LANES]
                t_ref[pl.ds(row + 16, 16), :] = both[:, LANES:]
            return carry

        lax.fori_loop(0, blocks, one, 0)

    def finish_group(g):
        wz = wz_ref[...]
        for part in range(2):
            cols = [t_ref[pl.ds(part * 8 + k, RANK, stride=16), :] for k in range(8)]
            y = nn(jnp.concatenate([q.astype(BF16) for q in cols], axis=1), wz)
            if part == 0:
                hsend[g, 1] = y[:, :LANES].astype(BF16)
                part_of[2 * me + g, :, :LANES] = y[:, LANES:].astype(BF16)
            else:
                part_of[2 * me + g, :, LANES:] = y[:, :LANES].astype(BF16)
                hsend[g, 0] = y[:, LANES:].astype(BF16)

    def make_leaf(q):
        below = jnp.where(sp > 0, hrecv[q, 0].astype(F32), 0.0)
        above = jnp.where(sp < count - 1, hrecv[q, 1].astype(F32), 0.0)
        leaf[q, :, :LANES] = (part_of[q, :, :LANES].astype(F32) + below).astype(BF16)
        leaf[q, :, LANES:] = (part_of[q, :, LANES:].astype(F32) + above).astype(BF16)

    restrict_group(0)
    small[2].wait()
    finish_group(0)
    pl.semaphore_wait(barrier, len(targets))
    early = piece_copies(0)
    for c in early:
        c.start()
    restrict_group(1)
    finish_group(1)
    late = piece_copies(1)
    for c in late:
        c.start()
    small[3].wait()
    skt[...] = jnp.concatenate([sk_ref[x] for x in range(sk_ref.shape[0])], axis=1)
    for c in early + late:
        c.wait()
    for q in range(2 * shots):
        make_leaf(q)

    p0 = leaf[pair_ref[base + 2 * odd]]
    p1 = leaf[pair_ref[base + 2 * odd + 1]]
    sk = skt[...]

    def scatter(part):
        out = []
        for d in owner_offsets:
            peer = near(d[1], d[2])
            src_rows = m_ref.at[part, pl.ds(pl.multiple_of(peer * rows, rows), rows)]
            out.append(
                remote(
                    src_rows, rs.at[part, o], rss.at[part, slot(d)], rsr.at[part, slot(d)],
                    group_peer(d),
                )
            )
        for c in out:
            c.start()
        rs[part, o] = m_ref[part, pl.ds(pl.multiple_of(o * rows, rows), rows), :]
        return out

    def along(part, copies):
        for c in copies:
            c.wait()
        total = rs[part, 0]
        for k in range(1, owners):
            total = total + rs[part, k]
        red[part] = total
        out = [
            remote(
                red.at[part], zb.at[part, z], zs.at[part, d - 1], zr.at[part, d - 1],
                depth_peer(d),
            )
            for d in depth_offsets
        ]
        for c in out:
            c.start()
        zb[part, z] = total
        return out

    def spread(part, copies):
        for c in copies:
            c.wait()
        total = zb[part, 0]
        for k in range(1, depth):
            total = total + zb[part, k]
        fin[part] = total
        out = [
            remote(
                fin.at[part], ga.at[part, line], gs.at[part, slot(d)], gr.at[part, slot(d)],
                group_peer(d),
            )
            for d in group_offsets
        ]
        for c in out:
            c.start()
        ga[part, line] = total
        return out

    m_ref[0, 0:64, :] = nt(p0, jnp.concatenate([p0, sk], axis=0))
    m_ref[0, 64:128, :] = nt(p1, jnp.concatenate([p1, sk], axis=0))
    first = scatter(0)
    xx = leaf[pair_ref[base + 2 + odd]]
    q0 = leaf[pair_ref[base]]
    q1 = leaf[pair_ref[base + 1]]
    m_ref[1, 0:64, :] = nt(xx, jnp.concatenate([q0, q1], axis=0))
    m_ref[1, 64:128, :] = jnp.concatenate([nt(p0, p1), nt(p1, p0)], axis=1)
    other = scatter(1)
    first = along(0, first)
    other = along(1, other)
    first = spread(0, first)
    other = spread(1, other)
    for c in first:
        c.wait()
    per = RANK // rows

    def block(part, index):
        return jnp.concatenate([ga[part, index * per + k] for k in range(per)], axis=0)

    aug = [block(0, p) for p in range(4)]
    c = solve_all(aug)
    for cp in other:
        cp.wait()
    pair_cols, second_in = [], []
    for m in range(2):
        cc = jnp.concatenate([c[2 * m], c[2 * m + 1]], axis=1)
        a0, a1 = aug[2 * m], aug[2 * m + 1]
        mix = block(1, 2 * m + 1)
        h = two_by_two(a0[:, :RANK], mix[:, :RANK], mix[:, RANK:], a1[:, :RANK])
        x = jnp.concatenate([a0[:, RANK:], a1[:, RANK:]], axis=0)
        second_in.append(gram_and_cross(cc, h, x, scaling))
        pair_cols.append(cc)
    k = jnp.concatenate([block(1, 0), block(1, 2)], axis=0)
    g10 = twice * exact_nt(exact_nn(pair_cols[1], k), pair_cols[0])
    g01 = jnp.transpose(g10)
    d = solve_all(second_in)
    dd = jnp.concatenate(d, axis=1)
    b0, b1 = second_in
    hm = two_by_two(b0[:, :RANK], g01, g10, b1[:, :RANK])
    x = jnp.concatenate([b0[:, RANK:], b1[:, RANK:]], axis=0)
    quad = twice * jnp.concatenate([nn(d[m], pair_cols[m]) for m in range(2)], axis=1)
    third = solve_all([gram_and_cross(dd, hm, x, scaling)], 8)
    u_ref[...] = scaling * exact_nn(third[0], quad, 2)
    width = out_ref.shape[1]
    partner = shots - 1 - me
    us[...] = u_ref[pl.ds(pl.multiple_of(partner * width, width), width), :].astype(BF16)
    trade = remote(us, ur, uss, usr, (partner, sp))
    trade.start()
    u = u_ref[pl.ds(pl.multiple_of(me * width, width), width), :].astype(BF16)
    total = None
    for p in range(4):
        term = nn(u[:, RANK * p : RANK * p + RANK], leaf[pair_ref[base + p]])
        total = term if total is None else total + term
    trade.wait()
    v = ur[...]
    for p in range(4):
        total = total + nn(v[:, RANK * p : RANK * p + RANK], leaf[pair_ref[4 - base + p]])
    for i in range(out_ref.shape[0]):
        out_ref[i] = total[:, RANK * i : RANK * i + RANK].astype(BF16)


def body(depth, probes, sources, sketch, pairing):
    groups, rank, steps, fine_x, fine_y, fine_z = probes.shape
    shots = lax.axis_size("shots")
    space = lax.axis_size("space")
    owners = space // depth
    wxy, wz = weight_tables(fine_x, fine_y, fine_z)
    fine_xy = fine_x * fine_y
    chunk = 16
    rows = LANES // owners
    group = 2 * owners
    dma = pltpu.SemaphoreType.DMA
    vmem = pltpu.VMEM
    scaling = math.sqrt(fine_x // 4 * space * 64 / rank)
    out_shape = (fine_x // 4, rank // shots, 64)
    return pl.pallas_call(
        functools.partial(kernel, scaling, shots, depth, owners),
        in_specs=[pl.BlockSpec(memory_space=pl.ANY)] * 5
        + [pl.BlockSpec(memory_space=pltpu.SMEM)],
        out_specs=pl.BlockSpec(memory_space=pltpu.VMEM),
        out_shape=pltpu.VMEM(out_shape, BF16),
        scratch_shapes=[
            vmem((groups, rank, steps, fine_xy, fine_z), BF16),
            vmem((groups, steps, fine_xy, fine_z), BF16),
            vmem(wxy.shape, BF16),
            vmem(wz.shape, BF16),
            vmem(sketch.shape, BF16),
            dma((groups, rank // chunk)),
            dma((4,)),
            vmem((rank * 16, LANES), F32),
            vmem((groups * shots, rank, 256), BF16),
            vmem((groups, 2, rank, LANES), BF16),
            vmem((groups * shots, 2, rank, LANES), BF16),
            vmem((groups * shots, rank, 256), BF16),
            vmem((rank, 256), BF16),
            vmem((2, LANES, LANES), F32),
            vmem((2, owners, rows, LANES), F32),
            vmem((2, rows, LANES), F32),
            vmem((2, depth, rows, LANES), F32),
            vmem((2, rows, LANES), F32),
            vmem((2, group, rows, LANES), F32),
            vmem((rank // shots, 256), BF16),
            vmem((rank // shots, 256), BF16),
            vmem((rank, 256), F32),
            dma((groups, 2, shots)), dma((groups, 2, shots)),
            dma((groups, shots - 1)), dma((groups, shots - 1)),
            dma((2, owners - 1)), dma((2, owners - 1)),
            dma((2, depth - 1)), dma((2, depth - 1)),
            dma((2, group - 1)), dma((2, group - 1)),
            dma, dma,
        ],
        compiler_params=pltpu.CompilerParams(collective_id=0, has_side_effects=True),
        name="merge",
    )(
        probes.reshape(groups, rank, steps, fine_xy, fine_z),
        sources.reshape(groups, steps, fine_xy, fine_z),
        jnp.asarray(wxy),
        jnp.asarray(wz),
        sketch,
        pairing,
    )


def solution(mesh):
    in_specs = (
        P("shots", None, None, "space", None, None),
        P("shots", None, "space", None, None),
        P("space", None, None),
        P(),
    )
    out_specs = P("space", "shots", None)
    depth = 8 if mesh.shape["space"] == 64 else 2
    return jax.shard_map(
        functools.partial(body, depth),
        mesh=mesh, in_specs=in_specs, out_specs=out_specs, check_vma=False,
    )
```

```python
import functools
import math

import jax
import jax.numpy as jnp
import numpy as np
from jax import lax
from jax.experimental import pallas as pl
from jax.experimental.pallas import tpu as pltpu
from jax.sharding import PartitionSpec as P

MESH = pl.DeviceIdType.MESH
F32 = jnp.float32
BF16 = jnp.bfloat16
RANK = 64
LANES = 128


def spline_weight(distance):
    s = np.abs(distance / 4.0)
    inner = 2.0 / 3.0 - s**2 + 0.5 * s**3
    outer = np.maximum(2.0 - s, 0.0) ** 3 / 6.0
    return np.where(s < 1.0, inner, outer) / 4.0


def weight_tables(fine_x, fine_y, fine_z):
    coarse_x, coarse_y, coarse_z = fine_x // 4 + 4, fine_y // 4, fine_z // 4
    jx, jy, jz = np.arange(fine_x), np.arange(fine_y), np.arange(fine_z)
    ix, iy, iz = np.arange(coarse_x) - 2, np.arange(coarse_y), np.arange(coarse_z)
    wx = spline_weight(jx[None, :] + 0.5 - 4 * ix[:, None] - 2)
    wy = spline_weight(jy[None, :] + 0.5 - 4 * iy[:, None] - 2)
    wz = spline_weight(jz[:, None] + 0.5 - 4 * iz[None, :] - 2)
    wxy = np.einsum("ij,de->idje", wx, wy).reshape(coarse_x * coarse_y, fine_x * fine_y)
    wxy = np.concatenate([wxy, wxy], axis=1).astype(np.float32)
    high = wxy.astype(BF16)
    low = (wxy - high.astype(np.float32)).astype(BF16)
    side = 8
    block = np.zeros((side, fine_z, side, coarse_z), np.float32)
    for i in range(side):
        block[i, :, i, :] = wz
    block = block.reshape(side * fine_z, side * coarse_z).astype(BF16)
    return np.concatenate([high, low], axis=0), block


def nt(a, b):
    return lax.dot_general(
        a, b, (((1,), (1,)), ((), ())), preferred_element_type=F32
    )


def nn(a, b):
    return jnp.dot(a, b, preferred_element_type=F32)


def from_row(x, i):
    return jnp.take_along_axis(x, jnp.full((8, LANES), i, jnp.int32), axis=0)


def eliminate(mats, width):
    sub = lax.broadcasted_iota(jnp.int32, (8, LANES), 0)
    for kb in range(0, RANK, width):
        v0, off = kb // 8, kb % 8
        for w in mats:
            cols = [
                [jnp.broadcast_to(w[v][:, kb + j : kb + j + 1], (8, LANES)) for v in range(8)]
                for j in range(width)
            ]
            r = [from_row(w[v0], off + i) for i in range(width)]
            e = [[from_row(cols[j][v0], off + i) for j in range(width)] for i in range(width)]
            for i in range(width):
                inv = 1.0 / e[i][i]
                r[i] = r[i] * inv
                for j in range(i + 1, width):
                    e[i][j] = e[i][j] * inv
                for k in range(width):
                    if k != i:
                        f = e[k][i]
                        r[k] = r[k] - f * r[i]
                        for j in range(i + 1, width):
                            e[k][j] = e[k][j] - f * e[i][j]
            for v in range(8):
                new = w[v]
                for j in range(width):
                    new = new - cols[j][v] * r[j]
                if v == v0:
                    for i in range(width):
                        new = jnp.where(sub == off + i, r[i], new)
                w[v] = new


def solve_all(mats, width=4):
    row = lax.broadcasted_iota(jnp.int32, (RANK, LANES), 0)
    lane = lax.broadcasted_iota(jnp.int32, (RANK, LANES), 1)
    diagonal = row == lane
    work = []
    for w in mats:
        trace = jnp.sum(jnp.where(diagonal, w, 0.0), axis=(0, 1), keepdims=True)
        ridge = 0.01 * trace / RANK + 1e-06
        w = jnp.where(diagonal, w + ridge, w)
        work.append([w[8 * v : 8 * v + 8] for v in range(8)])
    eliminate(work, width)
    out = []
    for w in work:
        full = jnp.concatenate(w, axis=0)
        out.append(jnp.transpose(full)[RANK:].astype(BF16))
    return out


def split(x, terms):
    out = []
    for _ in range(terms - 1):
        part = x.astype(BF16)
        out.append(part)
        x = x - part.astype(F32)
    out.append(x.astype(BF16))
    return out


def exact_nn(c, x, terms=3):
    return nn(jnp.concatenate([c] * terms, axis=1), jnp.concatenate(split(x, terms), axis=0))


def exact_nt(x, c, terms=3):
    return nt(jnp.concatenate(split(x, terms), axis=1), jnp.concatenate([c] * terms, axis=1))


def gram_and_cross(c, h, x, scaling):
    both = exact_nn(c, jnp.concatenate([h, x], axis=1))
    gm = exact_nt(both[:, :LANES], c)
    return jnp.concatenate([(scaling * scaling) * gm, scaling * both[:, LANES:]], axis=1)


def two_by_two(a, b, c, d):
    return jnp.concatenate(
        [jnp.concatenate([a, b], axis=1), jnp.concatenate([c, d], axis=1)], axis=0
    )


def kernel(
    scaling, shots, depth, owners,
    p_hbm, s_hbm, wxy_hbm, wz_hbm, sk_hbm, pair_ref,
    out_ref,
    p_ref, s_ref, wxy_ref, wz_ref, sk_ref, psem, csem,
    t_ref, part_of, hsend, hrecv, leaf, skt,
    m_ref, rs, red, zb, fin, ga, us, ur, u_ref,
    hs, hr, ys, yr, rss, rsr, zs, zr, gs, gr, uss, usr,
):
    chunk = 16
    blocks = RANK // chunk

    def load(g, i):
        at = pl.ds(i * chunk, chunk)
        return pltpu.make_async_copy(p_hbm.at[g, at], p_ref.at[g, at], psem.at[g, i])

    small = [
        pltpu.make_async_copy(src, dst, csem.at[i])
        for i, (src, dst) in enumerate(
            [(s_hbm, s_ref), (wxy_hbm, wxy_ref), (wz_hbm, wz_ref), (sk_hbm, sk_ref)]
        )
    ]
    small[0].start()
    small[1].start()
    for i in range(blocks):
        load(0, i).start()
    small[2].start()
    for i in range(blocks):
        load(1, i).start()
    small[3].start()
    me = lax.axis_index("shots")
    sp = lax.axis_index("space")
    count = depth * owners
    z = sp // owners
    o = lax.rem(sp, owners)
    right = lax.rem(sp + 1, count)
    left = lax.rem(sp + count - 1, count)
    half = me // 2
    odd = lax.rem(me, 2)
    base = 4 * half
    group = 2 * owners
    line = odd * owners + o
    rows = LANES // owners
    twice = scaling * scaling

    across = owners // 2
    at_x = o // 2
    core = lax.rem(o, 2)

    def ring(d, size):
        return min(d, size - d)

    def near(dx, dc):
        return lax.rem(at_x + dx, across) * 2 + lax.rem(core + dc, 2)

    group_offsets = sorted(
        [(dy, dx, dc) for dy in range(2) for dx in range(across) for dc in range(2)][1:],
        key=lambda d: (-d[0] - ring(d[1], across), -d[2]),
    )
    owner_offsets = [d for d in group_offsets if d[0] == 0]
    depth_offsets = sorted(range(1, depth), key=lambda d: -ring(d, depth))
    shot_offsets = sorted(range(shots), key=lambda d: -ring(d, shots))

    def slot(offset):
        dy, dx, dc = offset
        return dy * owners + dx * 2 + dc - 1

    def depth_peer(d):
        return (me, lax.rem(z + d, depth) * owners + o)

    def shot_peer(d):
        return (lax.rem(me + d, shots), sp)

    def group_peer(offset):
        dy, dx, dc = offset
        return (2 * half + lax.rem(odd + dy, 2), z * owners + near(dx, dc))

    barrier = pltpu.get_barrier_semaphore()

    targets = [(lax.rem(me + d, shots), side) for d in shot_offsets for side in (left, right)]
    targets += [depth_peer(d) for d in depth_offsets]
    targets += [shot_peer(d) for d in shot_offsets if d]
    targets += [group_peer(d) for d in group_offsets]
    for target in targets:
        pl.semaphore_signal(barrier, inc=1, device_id=target, device_id_type=MESH)

    def remote(src, dst, ssem, rsem, target):
        return pltpu.make_async_remote_copy(
            src_ref=src, dst_ref=dst, send_sem=ssem, recv_sem=rsem,
            device_id=target, device_id_type=MESH,
        )

    def piece_copies(g):
        mine = part_of.at[2 * me + g]
        out = []
        for d in shot_offsets:
            shot = lax.rem(me + d, shots)
            for side, peer in enumerate((right, left)):
                out.append(
                    remote(
                        hsend.at[g, side], hrecv.at[2 * me + g, side],
                        hs.at[g, side, d], hr.at[g, side, d], (shot, peer),
                    )
                )
            if d:
                out.append(remote(mine, mine, ys.at[g, d - 1], yr.at[g, d - 1], (shot, sp)))
        return out

    small[0].wait()
    small[1].wait()
    wxy = wxy_ref[...]

    def restrict_group(g):
        src = s_ref[g].reshape(256, LANES)

        def one(i, carry):
            load(g, i).wait()
            for a in range(0, chunk, 2):
                at = i * chunk + a
                first = p_ref[g, at].reshape(256, LANES) * src
                other = p_ref[g, at + 1].reshape(256, LANES) * src
                both = nn(wxy, jnp.concatenate([first, other], axis=1))
                both = both[:16] + both[16:]
                row = pl.multiple_of(at * 16, 32)
                t_ref[pl.ds(row, 16), :] = both[:, :LANES]
                t_ref[pl.ds(row + 16, 16), :] = both[:, LANES:]
            return carry

        lax.fori_loop(0, blocks, one, 0)

    def finish_group(g):
        wz = wz_ref[...]
        for part in range(2):
            cols = [t_ref[pl.ds(part * 8 + k, RANK, stride=16), :] for k in range(8)]
            y = nn(jnp.concatenate([q.astype(BF16) for q in cols], axis=1), wz)
            if part == 0:
                hsend[g, 1] = y[:, :LANES].astype(BF16)
                part_of[2 * me + g, :, :LANES] = y[:, LANES:].astype(BF16)
            else:
                part_of[2 * me + g, :, LANES:] = y[:, :LANES].astype(BF16)
                hsend[g, 0] = y[:, LANES:].astype(BF16)

    def leaf_of(q):
        below = jnp.where(sp > 0, hrecv[q, 0].astype(F32), 0.0)
        above = jnp.where(sp < count - 1, hrecv[q, 1].astype(F32), 0.0)
        lead = (part_of[q, :, :LANES].astype(F32) + below).astype(BF16)
        tail = (part_of[q, :, LANES:].astype(F32) + above).astype(BF16)
        return jnp.concatenate([lead, tail], axis=1)

    restrict_group(0)
    small[2].wait()
    finish_group(0)
    pl.semaphore_wait(barrier, len(targets))
    early = piece_copies(0)
    for c in early:
        c.start()
    restrict_group(1)
    finish_group(1)
    late = piece_copies(1)
    for c in late:
        c.start()
    small[3].wait()
    skt[...] = jnp.concatenate([sk_ref[x] for x in range(sk_ref.shape[0])], axis=1)
    for c in early + late:
        c.wait()

    p0 = leaf_of(pair_ref[base + 2 * odd])
    p1 = leaf_of(pair_ref[base + 2 * odd + 1])
    sk = skt[...]

    def scatter(part):
        out = []
        for d in owner_offsets:
            peer = near(d[1], d[2])
            src_rows = m_ref.at[part, pl.ds(pl.multiple_of(peer * rows, rows), rows)]
            out.append(
                remote(
                    src_rows, rs.at[part, o], rss.at[part, slot(d)], rsr.at[part, slot(d)],
                    group_peer(d),
                )
            )
        for c in out:
            c.start()
        rs[part, o] = m_ref[part, pl.ds(pl.multiple_of(o * rows, rows), rows), :]
        return out

    def along(part, copies):
        for c in copies:
            c.wait()
        total = rs[part, 0]
        for k in range(1, owners):
            total = total + rs[part, k]
        red[part] = total
        out = [
            remote(
                red.at[part], zb.at[part, z], zs.at[part, d - 1], zr.at[part, d - 1],
                depth_peer(d),
            )
            for d in depth_offsets
        ]
        for c in out:
            c.start()
        zb[part, z] = total
        return out

    def spread(part, copies):
        for c in copies:
            c.wait()
        total = zb[part, 0]
        for k in range(1, depth):
            total = total + zb[part, k]
        fin[part] = total
        out = [
            remote(
                fin.at[part], ga.at[part, line], gs.at[part, slot(d)], gr.at[part, slot(d)],
                group_peer(d),
            )
            for d in group_offsets
        ]
        for c in out:
            c.start()
        ga[part, line] = total
        return out

    m_ref[0, 0:64, :] = nt(p0, jnp.concatenate([p0, sk], axis=0))
    m_ref[0, 64:128, :] = nt(p1, jnp.concatenate([p1, sk], axis=0))
    first = scatter(0)
    for p in range(2 * shots):
        leaf[p] = leaf_of(pair_ref[p])
    xx = leaf[base + 2 + odd]
    q0 = leaf[base]
    q1 = leaf[base + 1]
    m_ref[1, 0:64, :] = nt(xx, jnp.concatenate([q0, q1], axis=0))
    m_ref[1, 64:128, :] = jnp.concatenate([nt(p0, p1), nt(p1, p0)], axis=1)
    other = scatter(1)
    first = along(0, first)
    other = along(1, other)
    first = spread(0, first)
    other = spread(1, other)
    for c in first:
        c.wait()
    per = RANK // rows

    def block(part, index):
        return jnp.concatenate([ga[part, index * per + k] for k in range(per)], axis=0)

    aug = [block(0, p) for p in range(4)]
    c = solve_all(aug)
    for cp in other:
        cp.wait()
    pair_cols, second_in = [], []
    for m in range(2):
        cc = jnp.concatenate([c[2 * m], c[2 * m + 1]], axis=1)
        a0, a1 = aug[2 * m], aug[2 * m + 1]
        mix = block(1, 2 * m + 1)
        h = two_by_two(a0[:, :RANK], mix[:, :RANK], mix[:, RANK:], a1[:, :RANK])
        x = jnp.concatenate([a0[:, RANK:], a1[:, RANK:]], axis=0)
        second_in.append(gram_and_cross(cc, h, x, scaling))
        pair_cols.append(cc)
    k = jnp.concatenate([block(1, 0), block(1, 2)], axis=0)
    g10 = twice * exact_nt(exact_nn(pair_cols[1], k), pair_cols[0])
    g01 = jnp.transpose(g10)
    d = solve_all(second_in)
    dd = jnp.concatenate(d, axis=1)
    b0, b1 = second_in
    hm = two_by_two(b0[:, :RANK], g01, g10, b1[:, :RANK])
    x = jnp.concatenate([b0[:, RANK:], b1[:, RANK:]], axis=0)
    quad = twice * jnp.concatenate([nn(d[m], pair_cols[m]) for m in range(2)], axis=1)
    third = solve_all([gram_and_cross(dd, hm, x, scaling)], 8)
    u_ref[...] = scaling * exact_nn(third[0], quad, 2)
    width = out_ref.shape[1]
    partner = shots - 1 - me
    us[...] = u_ref[pl.ds(pl.multiple_of(partner * width, width), width), :].astype(BF16)
    trade = remote(us, ur, uss, usr, (partner, sp))
    trade.start()
    u = u_ref[pl.ds(pl.multiple_of(me * width, width), width), :].astype(BF16)
    total = None
    for p in range(4):
        term = nn(u[:, RANK * p : RANK * p + RANK], leaf[base + p])
        total = term if total is None else total + term
    trade.wait()
    v = ur[...]
    for p in range(4):
        total = total + nn(v[:, RANK * p : RANK * p + RANK], leaf[4 - base + p])
    for i in range(out_ref.shape[0]):
        out_ref[i] = total[:, RANK * i : RANK * i + RANK].astype(BF16)


def body(depth, probes, sources, sketch, pairing):
    groups, rank, steps, fine_x, fine_y, fine_z = probes.shape
    shots = lax.axis_size("shots")
    space = lax.axis_size("space")
    owners = space // depth
    wxy, wz = weight_tables(fine_x, fine_y, fine_z)
    fine_xy = fine_x * fine_y
    chunk = 16
    rows = LANES // owners
    group = 2 * owners
    dma = pltpu.SemaphoreType.DMA
    vmem = pltpu.VMEM
    scaling = math.sqrt(fine_x // 4 * space * 64 / rank)
    out_shape = (fine_x // 4, rank // shots, 64)
    return pl.pallas_call(
        functools.partial(kernel, scaling, shots, depth, owners),
        in_specs=[pl.BlockSpec(memory_space=pl.ANY)] * 5
        + [pl.BlockSpec(memory_space=pltpu.SMEM)],
        out_specs=pl.BlockSpec(memory_space=pltpu.VMEM),
        out_shape=pltpu.VMEM(out_shape, BF16),
        scratch_shapes=[
            vmem((groups, rank, steps, fine_xy, fine_z), BF16),
            vmem((groups, steps, fine_xy, fine_z), BF16),
            vmem(wxy.shape, BF16),
            vmem(wz.shape, BF16),
            vmem(sketch.shape, BF16),
            dma((groups, rank // chunk)),
            dma((4,)),
            vmem((rank * 16, LANES), F32),
            vmem((groups * shots, rank, 256), BF16),
            vmem((groups, 2, rank, LANES), BF16),
            vmem((groups * shots, 2, rank, LANES), BF16),
            vmem((groups * shots, rank, 256), BF16),
            vmem((rank, 256), BF16),
            vmem((2, LANES, LANES), F32),
            vmem((2, owners, rows, LANES), F32),
            vmem((2, rows, LANES), F32),
            vmem((2, depth, rows, LANES), F32),
            vmem((2, rows, LANES), F32),
            vmem((2, group, rows, LANES), F32),
            vmem((rank // shots, 256), BF16),
            vmem((rank // shots, 256), BF16),
            vmem((rank, 256), F32),
            dma((groups, 2, shots)), dma((groups, 2, shots)),
            dma((groups, shots - 1)), dma((groups, shots - 1)),
            dma((2, owners - 1)), dma((2, owners - 1)),
            dma((2, depth - 1)), dma((2, depth - 1)),
            dma((2, group - 1)), dma((2, group - 1)),
            dma, dma,
        ],
        compiler_params=pltpu.CompilerParams(collective_id=0, has_side_effects=True),
        name="merge",
    )(
        probes.reshape(groups, rank, steps, fine_xy, fine_z),
        sources.reshape(groups, steps, fine_xy, fine_z),
        jnp.asarray(wxy),
        jnp.asarray(wz),
        sketch,
        pairing,
    )


def solution(mesh):
    in_specs = (
        P("shots", None, None, "space", None, None),
        P("shots", None, "space", None, None),
        P("space", None, None),
        P(),
    )
    out_specs = P("space", "shots", None)
    depth = 8 if mesh.shape["space"] == 64 else 2
    return jax.shard_map(
        functools.partial(body, depth),
        mesh=mesh, in_specs=in_specs, out_specs=out_specs, check_vma=False,
    )
```
